256 devices in a mesh: grid: 64 (over y, z, core), rep: 4 (over x).
Axes of the slice: x: 4, y: 4, z: 8, core: 2. Of those that a mesh axis runs over, the one named last changes fastest.
Arguments:
- integrals: bfloat16 [131072, 512], P(('grid', 'rep')), may hold values from -6 to 6
- green_occ: bfloat16 [512, 16384], P(None, 'grid'), may hold values from -0.25 to 0.25
- tile_panels: int32 [1024, 16], P(('grid', 'rep')), may hold values from 0 to 63, all different within a row; in each aligned block of 4 rows (0 to 3, 4 to 7, ...) at most 2 rows name the same one
- virtual_blocks: bfloat16 [64, 16, 256, 256], P('grid', 'rep'), may hold values from -0.0234375 to 0.0234375
Outputs:
- response_blocks: float32 [64, 128, 256], P('grid', 'rep')
The draws below stay inside these ranges and needn't reach their ends.
Inputs may be any that keep to these rules, and one draw needn't show every extreme that they name: `tile_panels`: each row lists 16 different panels. In each aligned block of 4 rows (the tiles of one device) no panel is listed by more than 2 rows, and some panel is listed by exactly 2 rows.
All inputs are finite; a program needn't handle non-finite values.
Results may differ from the reference program's by a relative error of at most 0.0029.
Values may be sent and summed in bfloat16 or wider, within the bound.
A program may use at most 128 MiB of HBM per device.

```python
import math
import jax
import jax.numpy as jnp
import numpy as np
from jax import lax

K = 512
W = 256
C = 256
TR = 128
NTD = 4
CAP = 2
NSEL = 16
NB = 16
TILES = 1024
LAM = 16384
ROWS = 131072
N_GRID = 64


def steps_of(key, shape, cuts, low, largest):
    def one(position, shards_of):
        steps = jax.random.uniform(jax.random.fold_in(jax.random.fold_in(key, 6), position), (shards_of,), jnp.float32, low / len(cuts), largest / len(cuts))
        return jnp.repeat(jnp.exp(steps), shape[position] // shards_of).reshape((-1,) + (1,) * (len(shape) - position - 1))

    loudness = one(*cuts[0])
    for cut in cuts[1:]:
        loudness = loudness * one(*cut)
    return loudness


def deal_out(rng, own, number, rows, amount, top, limit, lean):
    ranking = jax.random.permutation(rng, amount)
    packed, ordinary = portions_of(amount, rows * top, limit, lean, True), portions_of(amount, rows * top, limit, lean, False)
    places = jnp.arange(amount)

    def named(sizes, rotation):
        used = int((sizes > 0).sum())
        fixed = max(1, used // 4)
        shifted = fixed + (places - fixed + rotation * (used - fixed)) % max(1, amount - fixed)
        return jnp.zeros((amount,), jnp.int32).at[ranking[jnp.where(places < fixed, places, shifted)]].set(jnp.asarray(sizes, jnp.int32))

    sizes = jnp.where(number % 4 == 0, named(packed, number // 4), named(ordinary, number - number // 4 - 1))
    mixed = jax.random.permutation(jax.random.fold_in(own, 3), amount)
    source_of, taker = mixed[0:amount // 2 * 2:2], mixed[1:amount // 2 * 2:2]
    margin = jnp.minimum(sizes[source_of] - 1, limit - sizes[taker]) // 2
    margin = jnp.where((source_of == ranking[0]) | (taker == ranking[0]) | (sizes[taker] == 0), 0, jnp.maximum(margin, 0))
    shifted = jax.random.randint(jax.random.fold_in(own, 4), (amount // 2,), 0, 1 << 20) % (margin + 1)
    sizes = sizes.at[source_of].add(-shifted).at[taker].add(shifted)
    labels = jnp.searchsorted(jnp.cumsum(sizes), jnp.arange(rows * top), side="right").astype(jnp.int32)
    grid = labels.reshape(top, rows).T
    grid = grid[jax.random.permutation(jax.random.fold_in(own, 1), rows)]
    rotation = jax.random.randint(jax.random.fold_in(own, 2), (rows, 1), 0, top)
    return jnp.take_along_axis(grid, (jnp.arange(top)[None, :] + rotation) % top, axis=1)


def portions_of(count, total, reach, skew, full):
    loads = [(1 << 20) // math.isqrt(standing ** skew) + 1 for standing in range(1, count + 1)]
    largest = reach if full else min(reach, max(-(-total // count), total * loads[0] // sum(loads)))
    least = 1 if total - largest >= count - 1 else 0
    counts, spare = [largest] + [least] * (count - 1), total - largest - least * (count - 1)
    while spare > 0:
        free = [i for i in range(1, count) if counts[i] < largest] or [i for i in range(1, count) if counts[i] < reach]
        pool, left = sum([loads[i] for i in free]), spare
        for i in free:
            more = min(reach - counts[i], max(1, left * loads[i] // pool), spare)
            counts[i] = counts[i] + more
            spare = spare - more
    return np.array(counts)


def normal_values(own_key, shape, scale, reach, shards=(), held_as=jnp.bfloat16):
    result = scale * jax.random.normal(own_key, shape, jnp.float32)
    if shards:
        result = result * steps_of(own_key, shape, shards, -0.22, 0.18)
    return jnp.clip(result, -reach, reach).astype(held_as)


def setup_inputs(seed: int = 0) -> dict:
    streams_of = jax.random.split(jax.random.key(seed), 5)
    integrals = normal_values(streams_of[0], (ROWS, K), 1.0, 6.0, ((0, 256),))
    green_occ = normal_values(streams_of[1], (K, LAM), K ** -0.5, 0.25, ((1, 64),))
    tile_panels_keys = jax.random.split(jax.random.fold_in(streams_of[2], 1), TILES // NTD)
    tile_panels_turns = jax.random.permutation(jax.random.fold_in(streams_of[2], 3), TILES // NTD)
    tile_panels = jax.vmap(lambda own, number: deal_out(jax.random.fold_in(streams_of[2], 2), own, number, NTD, N_GRID, NSEL, CAP, 2))(tile_panels_keys, tile_panels_turns).reshape((TILES, NSEL))
    virtual_blocks = normal_values(streams_of[3], (N_GRID, NB, W, C), (1.0 / (W * NSEL * NB) ** 0.5), 0.0234375, ((0, 64), (1, 4)))
    return dict(integrals=integrals, green_occ=green_occ, tile_panels=tile_panels, virtual_blocks=virtual_blocks)


def reference(integrals, green_occ, tile_panels, virtual_blocks):
    grid_count = virtual_blocks.shape[0]
    block_count = virtual_blocks.shape[1]
    tile_count = tile_panels.shape[0]
    panels = green_occ.astype(jnp.float32).reshape(K, grid_count, W)
    tile_stack = integrals.reshape(tile_count, TR, K)

    def accumulate(running, tile_index):
        tile_block = tile_stack[tile_index].astype(jnp.float32)
        chosen = tile_panels[tile_index]
        chosen_panels = jnp.take(panels, chosen, axis=1)
        products = jnp.einsum("tk,ksw->stw", tile_block, chosen_panels, precision=lax.Precision.HIGHEST)
        rounded = lax.optimization_barrier(products.astype(jnp.bfloat16))
        block_index = tile_index % block_count
        running = running.at[chosen, block_index].add(rounded.astype(jnp.float32))
        return running, None

    start_sums = jnp.zeros((grid_count, block_count, TR, W), jnp.float32)
    summed, _ = lax.scan(accumulate, start_sums, jnp.arange(tile_count, dtype=jnp.int32))
    return jnp.einsum("jbtw,jbwc->jtc", summed, virtual_blocks.astype(jnp.float32), precision=lax.Precision.HIGHEST)
```

```python
import jax
import jax.numpy as jnp
from jax import lax
from jax.experimental import pallas as pl
from jax.experimental.pallas import tpu as pltpu
from jax.sharding import PartitionSpec as P

NY, NZ, NC, NX = 4, 8, 2, 4
NP = NY * NC
F32, BF16 = jnp.float32, jnp.bfloat16


def body(a_hbm, g_hbm, tp_ref, v_hbm, out_ref,
         abuf, gbuf, tpbuf, vbuf, mask, part, stage, got, resp, xbuf,
         loc_sem, tp_s, tp_r, a_s, a_r, gz_s, gz_r, gx_s, gx_r, rs_s, rs_r, x_s, x_r):
    tiles, _, tr, _ = abuf.shape
    depth = gbuf.shape[1]
    half = tr // 2
    gi, r = lax.axis_index("grid"), lax.axis_index("rep")
    c, z, y = gi % NC, (gi // NC) % NZ, gi // (NC * NZ)
    me = y * NC + c

    def gid(yy, zz, cc):
        return (yy * NZ + zz) * NC + cc

    yl, yr, yo = (y + NY - 1) % NY, (y + 1) % NY, (y + 2) % NY
    partner = (gid(y, z, 1 - c), r)
    yp, ym = (gid(yr, z, c), r), (gid(yl, z, c), r)
    zp, zm = (gid(y, (z + 1) % NZ, c), r), (gid(y, (z + NZ - 1) % NZ, c), r)
    xs = [(gi, (r + d) % NX) for d in range(1, NX)]
    xp, xm = xs[0], xs[2]
    group = []
    for o in range(1, NP):
        q = (me + o) % NP
        group.append((gid(q // NC, z, q % NC), r))
    sends = []

    def send(src, dst, ss, rs, dev):
        copy = pltpu.make_async_remote_copy(
            src_ref=src, dst_ref=dst, send_sem=ss, recv_sem=rs,
            device_id=dev, device_id_type=pl.DeviceIdType.MESH)
        copy.start()
        sends.append(copy)

    def arrive(dst, ss, rs, dev):
        pltpu.make_async_remote_copy(
            src_ref=dst, dst_ref=dst, send_sem=ss, recv_sem=rs,
            device_id=dev, device_id_type=pl.DeviceIdType.MESH).wait_recv()

    local = [pltpu.make_async_copy(g_hbm, gbuf.at[z], loc_sem.at[tiles])]
    for l in range(tiles):
        local.append(pltpu.make_async_copy(a_hbm.at[l], abuf.at[l, me], loc_sem.at[l]))
    local.append(pltpu.make_async_copy(tp_ref, tpbuf.at[me], loc_sem.at[tiles + 1]))
    local.append(pltpu.make_async_copy(v_hbm, vbuf, loc_sem.at[tiles + 2]))
    for copy in local:
        copy.start()
    barrier = pltpu.get_barrier_semaphore()
    peers = group + [zp, zm] + xs
    for dev in peers:
        pl.semaphore_signal(barrier, inc=1, device_id=dev, device_id_type=pl.DeviceIdType.MESH)
    pl.semaphore_wait(barrier, len(peers))
    for copy in local:
        copy.wait()

    quarter = depth // 4
    par = r % 2

    def rows(parity, h):
        return pl.ds(pl.multiple_of((parity + 2 * h) * quarter, quarter), quarter)

    def g_send(way, k):
        d = k // 2
        zz = (z + NZ - d) % NZ if way == 0 else (z + d) % NZ
        h = k % 2 if k < 6 else way
        ref = gbuf.at[zz, rows(par, h)]
        send(ref, ref, gz_s.at[way, k], gz_r.at[way, k], zp if way == 0 else zm)

    def g_event(k):
        for way in (0, 1):
            d = k // 2 + 1
            zz = (z + NZ - d) % NZ if way == 0 else (z + d) % NZ
            h = k % 2 if k < 6 else way
            ref = gbuf.at[zz, rows(par, h)]
            arrive(ref, gz_s.at[way, k], gz_r.at[way, k], zp if way == 0 else zm)
            nxt = k + 2
            if nxt < 6:
                g_send(way, nxt)
            elif nxt in (6, 7) and h == way:
                g_send(way, 6)
            pidx = 6 if d == 4 else 2 * (d - 1) + way
            send(ref, ref, gx_s.at[h, pidx], gx_r.at[h, pidx], xp if h == 0 else xm)

    def g_side(pidx):
        d = pidx // 2 + 1
        zz = (z + NZ - d) % NZ if pidx % 2 == 0 else (z + d) % NZ
        for h in (0, 1):
            arrive(gbuf.at[zz, rows(1 - par, h)], gx_s.at[h, pidx], gx_r.at[h, pidx],
                   xp if h == 0 else xm)

    sl, sr, so = yl * NC + c, yr * NC + c, yo * NC + c
    ol, orr, oo, om = yl * NC + 1 - c, yr * NC + 1 - c, yo * NC + 1 - c, y * NC + 1 - c
    top, low = pl.ds(0, half), pl.ds(half, half)

    def a_send(l, slot, i, dev, cut=None):
        ref = abuf.at[l, slot] if cut is None else abuf.at[l, slot, cut]
        send(ref, ref, a_s.at[l, i], a_r.at[l, i], dev)

    def a_arrive(l, slot, i, dev, cut=None):
        ref = abuf.at[l, slot] if cut is None else abuf.at[l, slot, cut]
        arrive(ref, a_s.at[l, i], a_r.at[l, i], dev)

    def a_own(l):
        a_send(l, me, 0, yp)
        a_send(l, me, 1, ym)
        a_send(l, me, 4, partner)

    def a_hop(l):
        a_arrive(l, sl, 0, yp)
        a_send(l, sl, 2, yp, top)
        a_send(l, sl, 5, partner)
        a_arrive(l, sr, 1, ym)
        a_send(l, sr, 3, ym, low)
        a_send(l, sr, 6, partner)

    def a_far(l):
        a_arrive(l, so, 2, yp, top)
        a_send(l, so, 7, partner, top)
        a_arrive(l, so, 3, ym, low)
        a_send(l, so, 8, partner, low)

    def a_done(l):
        a_arrive(l, om, 4, partner)
        a_arrive(l, ol, 5, partner)
        a_arrive(l, orr, 6, partner)
        a_arrive(l, oo, 7, partner, top)
        a_arrive(l, oo, 8, partner, low)

    def masks():
        for o in range(1, NP):
            arrive(tpbuf.at[(me + NP - o) % NP], tp_s.at[o - 1], tp_r.at[o - 1], group[o - 1])
        tp = tpbuf[...].reshape(NP * 8, 128)
        lane = lax.broadcasted_iota(jnp.int32, (NP * 8, 128), 1)
        hit = jnp.zeros((NP * 8, 128), F32)
        for k in range(16):
            hit = hit + (tp[:, k:k + 1] == lane).astype(F32)
        row = lax.broadcasted_iota(jnp.int32, (128, NZ * 128), 0)
        col = lax.broadcasted_iota(jnp.int32, (128, NZ * 128), 1) // 128
        pick = (row == (y * NZ + col) * NC + c).astype(F32).astype(BF16)
        mask[...] = jnp.dot(hit.astype(BF16), pick, preferred_element_type=F32)

    def compute(l, dz):
        zz = (z + dz) % NZ
        lanes = pl.ds(pl.multiple_of(zz * 128, 128), 128)
        prod = jnp.dot(abuf[l].reshape(NP * tr, abuf.shape[3]), gbuf[zz],
                       preferred_element_type=F32).astype(BF16).astype(F32)
        total = None
        for s in range(NP):
            m = mask[pl.ds(s * 8 + l, 1), lanes]
            term = prod[s * tr:(s + 1) * tr] * jnp.concatenate([m, m], axis=1)
            total = term if total is None else total + term
        part[l, zz] = total

    def rs_step(l, t):
        for way in (0, 1):
            d = 4 - t
            zz = (z + d) % NZ if way == 0 else (z + NZ - d) % NZ
            dev = zp if way == 0 else zm
            cut = top if way == 0 else low
            if t == 0:
                stage[way, l, 0, cut] = part[l, zz, cut].astype(BF16)
                src, dst = stage.at[way, l, 0, cut], got.at[way, l, 0, cut]
            else:
                rs_wait(l, t - 1, way)
                if t == 1:
                    other = low if way == 0 else top
                    stage[way, l, 1, cut] = (part[l, zz, cut] + got[way, l, 0, cut].astype(F32)).astype(BF16)
                    stage[way, l, 1, other] = part[l, zz, other].astype(BF16)
                else:
                    stage[way, l, t] = (part[l, zz] + got[way, l, t - 1].astype(F32)).astype(BF16)
                src, dst = stage.at[way, l, t], got.at[way, l, t]
            send(src, dst, rs_s.at[way, l, t], rs_r.at[way, l, t], dev)

    def rs_wait(l, t, way):
        cut = top if way == 0 else low
        ref = got.at[way, l, t, cut] if t == 0 else got.at[way, l, t]
        arrive(ref, rs_s.at[way, l, t], rs_r.at[way, l, t], zp if way == 0 else zm)

    def finish(l):
        rs_wait(l, 3, 0)
        rs_wait(l, 3, 1)
        total = part[l, z] + got[0, l, 3].astype(F32) + got[1, l, 3].astype(F32)
        high = total.astype(BF16)
        rest = (total - high.astype(F32)).astype(BF16)
        value = (jnp.dot(high, vbuf[l], preferred_element_type=F32)
                 + jnp.dot(rest, vbuf[l], preferred_element_type=F32))
        resp[...] = value if l == 0 else resp[...] + value

    for k in range(2):
        for way in (0, 1):
            g_send(way, k)
    for o in range(1, NP):
        send(tpbuf.at[me], tpbuf.at[me], tp_s.at[o - 1], tp_r.at[o - 1], group[o - 1])
    a_own(0)
    a_own(1)
    g_event(0)
    g_event(1)
    a_hop(0)
    a_own(2)
    g_event(2)
    g_event(3)
    a_far(0)
    masks()
    a_hop(1)
    a_own(3)
    g_event(4)
    a_done(0)
    compute(0, 0)
    g_event(5)
    g_side(0)
    compute(0, -1 % NZ)
    g_side(1)
    compute(0, 1)
    a_far(1)
    g_event(6)
    g_side(2)
    compute(0, -2 % NZ)
    g_side(3)
    compute(0, 2)
    a_hop(2)
    g_side(4)
    compute(0, -3 % NZ)
    g_side(5)
    compute(0, 3)
    g_side(6)
    compute(0, 4)
    rs_step(0, 0)
    for l in range(1, tiles):
        a_done(l)
        compute(l, 4)
        rs_step(l, 0)
        if l + 1 < tiles:
            a_far(l + 1)
        compute(l, 3)
        compute(l, -3 % NZ)
        if l >= 2:
            rs_step(l - 2, 3)
        rs_step(l - 1, 1)
        compute(l, 2)
        compute(l, -2 % NZ)
        if l + 2 < tiles:
            a_hop(l + 2)
        compute(l, 1)
        compute(l, -1 % NZ)
        rs_step(l - 1, 2)
        if l >= 2:
            finish(l - 2)
        compute(l, 0)
    last = tiles - 1
    rs_step(last, 1)
    rs_step(last - 1, 3)
    rs_step(last, 2)
    finish(last - 1)
    rs_step(last, 3)
    finish(last)

    count = out_ref.shape[1]
    for d in range(1, NX):
        dst_r = (r + d) % NX
        send(resp.at[pl.ds(pl.multiple_of(dst_r * count, count), count)], xbuf.at[d - 1],
             x_s.at[d - 1], x_r.at[d - 1], xs[d - 1])
    total = resp[pl.ds(pl.multiple_of(r * count, count), count)]
    for d in range(1, NX):
        arrive(xbuf.at[d - 1], x_s.at[d - 1], x_r.at[d - 1], xs[d - 1])
        total = total + xbuf[d - 1]
    out_ref[0] = total
    for copy in sends:
        copy.wait_send()


def shards(integrals, green_occ, tile_panels, virtual_blocks):
    tiles = tile_panels.shape[0]
    tr = integrals.shape[0] // tiles
    depth, width = green_occ.shape
    cols = virtual_blocks.shape[3]
    tp = jnp.pad(tile_panels, ((0, 8 - tiles), (0, 128 - tile_panels.shape[1])), constant_values=-1)
    dma = pltpu.SemaphoreType.DMA
    anywhere = pl.BlockSpec(memory_space=pl.ANY)
    vmem = pl.BlockSpec(memory_space=pltpu.VMEM)
    return pl.pallas_call(
        body,
        out_shape=jax.ShapeDtypeStruct((1, tr // NX, cols), F32),
        in_specs=[anywhere, anywhere, vmem, anywhere],
        out_specs=vmem,
        scratch_shapes=[
            pltpu.VMEM((tiles, NP, tr, depth), BF16),
            pltpu.VMEM((NZ, depth, width), BF16),
            pltpu.VMEM((NP, 8, 128), jnp.int32),
            pltpu.VMEM((tiles, width, cols), BF16),
            pltpu.VMEM((NP * 8, NZ * 128), F32),
            pltpu.VMEM((tiles, NZ, tr, width), F32),
            pltpu.VMEM((2, tiles, 4, tr, width), BF16),
            pltpu.VMEM((2, tiles, 4, tr, width), BF16),
            pltpu.VMEM((tr, cols), F32),
            pltpu.VMEM((NX - 1, tr // NX, cols), F32),
            dma((tiles + 3,)),
            dma((NP - 1,)), dma((NP - 1,)),
            dma((tiles, 9)), dma((tiles, 9)),
            dma((2, 7)), dma((2, 7)),
            dma((2, 7)), dma((2, 7)),
            dma((2, tiles, 4)), dma((2, tiles, 4)),
            dma((NX - 1,)), dma((NX - 1,)),
        ],
        compiler_params=pltpu.CompilerParams(collective_id=0, has_side_effects=True),
    )(integrals.reshape(tiles, tr, depth), green_occ, tp, virtual_blocks[0])


def solution(mesh):
    in_specs = (
        P(("grid", "rep"), None),
        P(None, "grid"),
        P(("grid", "rep"), None),
        P("grid", "rep", None, None),
    )
    out_specs = P("grid", "rep", None)
    return jax.shard_map(shards, mesh=mesh, in_specs=in_specs, out_specs=out_specs, check_vma=False)
```

```python
import jax
import jax.numpy as jnp
from jax import lax
from jax.experimental import pallas as pl
from jax.experimental.pallas import tpu as pltpu
from jax.sharding import PartitionSpec as P

NY, NZ, NC, NX = 4, 8, 2, 4
NP = NY * NC
F32, BF16 = jnp.float32, jnp.bfloat16


def body(a_hbm, g_hbm, tp_hbm, v_hbm, out_ref,
         abuf, gbuf, tpbuf, vbuf, hits, mask, part, stage, got, resp, xbuf,
         loc_sem, tp_s, tp_r, a_s, a_r, gz_s, gz_r, gx_s, gx_r, rs_s, rs_r, x_s, x_r):
    tiles, _, tr, _ = abuf.shape
    depth = gbuf.shape[1]
    half = tr // 2
    gi, r = lax.axis_index("grid"), lax.axis_index("rep")
    c, z, y = gi % NC, (gi // NC) % NZ, gi // (NC * NZ)
    me = y * NC + c

    def gid(yy, zz, cc):
        return (yy * NZ + zz) * NC + cc

    yl, yr, yo = (y + NY - 1) % NY, (y + 1) % NY, (y + 2) % NY
    partner = (gid(y, z, 1 - c), r)
    yp, ym = (gid(yr, z, c), r), (gid(yl, z, c), r)
    zp, zm = (gid(y, (z + 1) % NZ, c), r), (gid(y, (z + NZ - 1) % NZ, c), r)
    xs = [(gi, (r + d) % NX) for d in range(1, NX)]
    xp, xm = xs[0], xs[2]
    group = []
    for o in range(1, NP):
        q = (me + o) % NP
        group.append((gid(q // NC, z, q % NC), r))
    sends = []

    def send(src, dst, ss, rs, dev):
        copy = pltpu.make_async_remote_copy(
            src_ref=src, dst_ref=dst, send_sem=ss, recv_sem=rs,
            device_id=dev, device_id_type=pl.DeviceIdType.MESH)
        copy.start()
        sends.append(copy)

    def arrive(dst, ss, rs, dev):
        pltpu.make_async_remote_copy(
            src_ref=dst, dst_ref=dst, send_sem=ss, recv_sem=rs,
            device_id=dev, device_id_type=pl.DeviceIdType.MESH).wait_recv()

    local = [pltpu.make_async_copy(g_hbm, gbuf.at[z], loc_sem.at[tiles])]
    for l in range(tiles):
        local.append(pltpu.make_async_copy(a_hbm.at[l], abuf.at[l, me], loc_sem.at[l]))
    local.append(pltpu.make_async_copy(tp_hbm, tpbuf.at[me], loc_sem.at[tiles + 1]))
    local.append(pltpu.make_async_copy(v_hbm, vbuf, loc_sem.at[tiles + 2]))
    for copy in local:
        copy.start()
    barrier = pltpu.get_barrier_semaphore()
    peers = group + [zp, zm] + [(gid(y, (z + d) % NZ, c), r) for d in (2, NZ - 2)] + xs
    for dev in peers:
        pl.semaphore_signal(barrier, inc=1, device_id=dev, device_id_type=pl.DeviceIdType.MESH)
    pl.semaphore_wait(barrier, len(peers))
    for copy in local:
        copy.wait()

    quarter = depth // 4
    par = r % 2

    def rows(parity, h):
        return pl.ds(pl.multiple_of((parity + 2 * h) * quarter, quarter), quarter)

    def toward(way, d):
        return (z + d) % NZ if way == 0 else (z + NZ - d) % NZ

    def z_dev(way, d):
        return (gid(y, toward(way, d), c), r)

    far = (2, 2, 1, 1, 4, 3, 3)
    jump = (2, 2, 1, 1, 2, 1, 1)

    def g_half(way, k):
        return way if k == 4 else (k + k // 5) % 2

    def g_send(way, k):
        ref = gbuf.at[toward(1 - way, far[k] - jump[k]), rows(par, g_half(way, k))]
        send(ref, ref, gz_s.at[way, k], gz_r.at[way, k], z_dev(way, jump[k]))

    def g_event(k):
        for way in (0, 1):
            h = g_half(way, k)
            ref = gbuf.at[toward(1 - way, far[k]), rows(par, h)]
            arrive(ref, gz_s.at[way, k], gz_r.at[way, k], z_dev(way, jump[k]))
            if k < 2:
                if h == way:
                    g_send(way, 4)
                g_send(way, 5 + h)
            send(ref, ref, gx_s.at[h, g_place(far[k], way)], gx_r.at[h, g_place(far[k], way)],
                 xp if h == 0 else xm)

    def g_place(d, way):
        return 6 if d == 4 else 2 * (d - 1) + way

    def g_side(d):
        for way in (0, 1) if d < 4 else (0,):
            for h in (0, 1):
                arrive(gbuf.at[toward(1 - way, d), rows(1 - par, h)], gx_s.at[h, g_place(d, way)],
                       gx_r.at[h, g_place(d, way)], xp if h == 0 else xm)

    sl, sr, so = yl * NC + c, yr * NC + c, yo * NC + c
    ol, orr, oo, om = yl * NC + 1 - c, yr * NC + 1 - c, yo * NC + 1 - c, y * NC + 1 - c
    top, low = pl.ds(0, half), pl.ds(half, half)

    def a_send(l, slot, i, dev, cut=None):
        ref = abuf.at[l, slot] if cut is None else abuf.at[l, slot, cut]
        send(ref, ref, a_s.at[l, i], a_r.at[l, i], dev)

    def a_arrive(l, slot, i, dev, cut=None):
        ref = abuf.at[l, slot] if cut is None else abuf.at[l, slot, cut]
        arrive(ref, a_s.at[l, i], a_r.at[l, i], dev)

    def a_own(l):
        a_send(l, me, 0, yp)
        a_send(l, me, 1, ym)
        a_send(l, me, 4, partner)

    def a_hop(l):
        a_arrive(l, sl, 0, yp)
        a_send(l, sl, 2, yp, top)
        a_send(l, sl, 5, partner)
        a_arrive(l, sr, 1, ym)
        a_send(l, sr, 3, ym, low)
        a_send(l, sr, 6, partner)

    def a_far(l):
        a_arrive(l, so, 2, yp, top)
        a_send(l, so, 7, partner, top)
        a_arrive(l, so, 3, ym, low)
        a_send(l, so, 8, partner, low)

    def a_done(l):
        a_arrive(l, om, 4, partner)
        a_arrive(l, ol, 5, partner)
        a_arrive(l, orr, 6, partner)
        a_arrive(l, oo, 7, partner, top)
        a_arrive(l, oo, 8, partner, low)

    def masks():
        for o in range(1, NP):
            arrive(tpbuf.at[(me + NP - o) % NP], tp_s.at[o - 1], tp_r.at[o - 1], group[o - 1])
        lane = lax.broadcasted_iota(jnp.int32, (tiles, 128), 1)
        hits[...] = jnp.zeros_like(hits)
        for s in range(NP):
            tp = tpbuf[s]
            hit = jnp.zeros((tiles, 128), F32)
            for k in range(tp.shape[1]):
                hit = hit + (tp[:, k:k + 1] == lane).astype(F32)
            hits[s, pl.ds(0, tiles)] = hit
        hit = hits[...].reshape(NP * 8, 128)
        row = lax.broadcasted_iota(jnp.int32, (128, NZ * 128), 0)
        col = lax.broadcasted_iota(jnp.int32, (128, NZ * 128), 1) // 128
        pick = (row == (y * NZ + col) * NC + c).astype(F32).astype(BF16)
        mask[...] = jnp.dot(hit.astype(BF16), pick, preferred_element_type=F32)

    def compute(l, *panels):
        for dz in panels:
            one_panel(l, dz)

    def one_panel(l, dz):
        zz = (z + dz % NZ) % NZ
        lanes = pl.ds(pl.multiple_of(zz * 128, 128), 128)
        prod = jnp.dot(abuf[l].reshape(NP * tr, abuf.shape[3]), gbuf[zz],
                       preferred_element_type=F32).astype(BF16).astype(F32)
        total = None
        for s in range(NP):
            m = mask[pl.ds(s * 8 + l, 1), lanes]
            term = prod[s * tr:(s + 1) * tr] * jnp.concatenate([m, m], axis=1)
            total = term if total is None else total + term
        part[l, zz] = total

    def rs_step(l, t):
        for way in (0, 1):
            d = 4 - t
            zz = (z + d) % NZ if way == 0 else (z + NZ - d) % NZ
            dev = zp if way == 0 else zm
            cut = top if way == 0 else low
            if t == 0:
                stage[way, l, 0, cut] = part[l, zz, cut].astype(BF16)
                src, dst = stage.at[way, l, 0, cut], got.at[way, l, 0, cut]
            else:
                rs_wait(l, t - 1, way)
                if t == 1:
                    other = low if way == 0 else top
                    stage[way, l, 1, cut] = (part[l, zz, cut] + got[way, l, 0, cut].astype(F32)).astype(BF16)
                    stage[way, l, 1, other] = part[l, zz, other].astype(BF16)
                else:
                    stage[way, l, t] = (part[l, zz] + got[way, l, t - 1].astype(F32)).astype(BF16)
                src, dst = stage.at[way, l, t], got.at[way, l, t]
            send(src, dst, rs_s.at[way, l, t], rs_r.at[way, l, t], dev)

    def rs_wait(l, t, way):
        cut = top if way == 0 else low
        ref = got.at[way, l, t, cut] if t == 0 else got.at[way, l, t]
        arrive(ref, rs_s.at[way, l, t], rs_r.at[way, l, t], zp if way == 0 else zm)

    def finish(l):
        rs_wait(l, 3, 0)
        rs_wait(l, 3, 1)
        total = part[l, z] + got[0, l, 3].astype(F32) + got[1, l, 3].astype(F32)
        high = total.astype(BF16)
        rest = (total - high.astype(F32)).astype(BF16)
        value = (jnp.dot(high, vbuf[l], preferred_element_type=F32)
                 + jnp.dot(rest, vbuf[l], preferred_element_type=F32))
        resp[...] = value if l == 0 else resp[...] + value

    for k in range(tiles):
        g_send(0, k)
        g_send(1, k)
        a_own(k)
    for o in range(1, NP):
        send(tpbuf.at[me], tpbuf.at[me], tp_s.at[o - 1], tp_r.at[o - 1], group[o - 1])
    a_hop(0)
    g_event(0)
    a_hop(1)
    g_event(1)
    g_event(2)
    a_hop(2)
    g_event(3)
    masks()
    a_hop(3)
    g_event(4)
    g_event(5)
    a_far(0)
    g_event(6)
    a_far(1)
    a_far(2)
    g_side(4)
    a_done(0)
    compute(0, 4)
    rs_step(0, 0)
    a_far(3)
    for l in range(1, tiles):
        a_done(l)
        compute(l, 4)
        rs_step(l, 0)
    g_side(3)
    for l in range(tiles):
        compute(l, 3, -3)
        rs_step(l, 1)
    g_side(2)
    for l in range(tiles):
        compute(l, 2, -2)
        rs_step(l, 2)
    g_side(1)
    for l in range(tiles):
        compute(l, 1, -1)
        rs_step(l, 3)
    for l in range(tiles):
        compute(l, 0)
        finish(l)

    count = out_ref.shape[1]
    for d in (2, 1, 3):
        dst_r = (r + d) % NX
        send(resp.at[pl.ds(pl.multiple_of(dst_r * count, count), count)], xbuf.at[d - 1],
             x_s.at[d - 1], x_r.at[d - 1], xs[d - 1])
    total = resp[pl.ds(pl.multiple_of(r * count, count), count)]
    for d in range(1, NX):
        arrive(xbuf.at[d - 1], x_s.at[d - 1], x_r.at[d - 1], xs[d - 1])
        total = total + xbuf[d - 1]
    out_ref[0] = total
    for copy in sends:
        copy.wait_send()


def shards(integrals, green_occ, tile_panels, virtual_blocks):
    tiles = tile_panels.shape[0]
    tr = integrals.shape[0] // tiles
    depth, width = green_occ.shape
    cols = virtual_blocks.shape[3]
    dma = pltpu.SemaphoreType.DMA
    anywhere = pl.BlockSpec(memory_space=pl.ANY)
    vmem = pl.BlockSpec(memory_space=pltpu.VMEM)
    return pl.pallas_call(
        body,
        out_shape=jax.ShapeDtypeStruct((1, tr // NX, cols), F32),
        in_specs=[anywhere] * 4,
        out_specs=vmem,
        scratch_shapes=[
            pltpu.VMEM((tiles, NP, tr, depth), BF16),
            pltpu.VMEM((NZ, depth, width), BF16),
            pltpu.VMEM((NP,) + tile_panels.shape, jnp.int32),
            pltpu.VMEM((tiles, width, cols), BF16),
            pltpu.VMEM((NP, 8, 128), F32),
            pltpu.VMEM((NP * 8, NZ * 128), F32),
            pltpu.VMEM((tiles, NZ, tr, width), F32),
            pltpu.VMEM((2, tiles, 4, tr, width), BF16),
            pltpu.VMEM((2, tiles, 4, tr, width), BF16),
            pltpu.VMEM((tr, cols), F32),
            pltpu.VMEM((NX - 1, tr // NX, cols), F32),
            dma((tiles + 3,)),
            dma((NP - 1,)), dma((NP - 1,)),
            dma((tiles, 9)), dma((tiles, 9)),
            dma((2, 7)), dma((2, 7)),
            dma((2, 7)), dma((2, 7)),
            dma((2, tiles, 4)), dma((2, tiles, 4)),
            dma((NX - 1,)), dma((NX - 1,)),
        ],
        compiler_params=pltpu.CompilerParams(collective_id=0, has_side_effects=True),
    )(integrals.reshape(tiles, tr, depth), green_occ, tile_panels, virtual_blocks[0])


def solution(mesh):
    in_specs = (
        P(("grid", "rep"), None),
        P(None, "grid"),
        P(("grid", "rep"), None),
        P("grid", "rep", None, None),
    )
    out_specs = P("grid", "rep", None)
    return jax.shard_map(shards, mesh=mesh, in_specs=in_specs, out_specs=out_specs, check_vma=False)
```
